32 devices in a mesh: dp: 8 (over z, x), tensor: 4 (over y, core).
Axes of the slice: x: 2, y: 2, z: 4, core: 2. Of those that a mesh axis runs over, the one named last changes fastest.
Arguments:
- tokens: bfloat16 [16384, 768], P(('dp', 'tensor')), may hold values from -6 to 6
- segments: int32 [8, 2048], P('dp'), may hold values from 0 to 7, never falling along the last dimension, each value on 1 to 1024 neighbouring positions
- block_perm: int32 [12], P('tensor'), may hold values from 0 to 1
- w_qkv: bfloat16 [3, 768, 768], P(None, None, 'tensor'), may hold values from -0.21875 to 0.21875
- b_qv: bfloat16 [2, 768], P(None, 'tensor'), may hold values from -3 to 3
- w_out: bfloat16 [768, 768], P('tensor'), may hold values from -2.5 to 2.5
- b_out: bfloat16 [768], replicated, may hold values from -3 to 3
- ln1_gain: bfloat16 [768], replicated, may hold values from 0.5 to 1.5
- ln1_bias: bfloat16 [768], replicated, may hold values from -3 to 3
- w_up: bfloat16 [768, 3072], P(None, 'tensor'), may hold values from -0.21875 to 0.21875
- b_up: bfloat16 [3072], P('tensor'), may hold values from -3 to 3
- w_down: bfloat16 [3072, 768], P('tensor'), may hold values from -0.109375 to 0.109375
- b_down: bfloat16 [768], replicated, may hold values from -3 to 3
- ln2_gain: bfloat16 [768], replicated, may hold values from 0.5 to 1.5
- ln2_bias: bfloat16 [768], replicated, may hold values from -3 to 3
- cotangent: bfloat16 [16384, 768], P(('dp', 'tensor')), may hold values from -6 to 6
Outputs:
- out: bfloat16 [16384, 768], P(('dp', 'tensor'))
- grad_tokens: bfloat16 [16384, 768], P(('dp', 'tensor'))
- grad_w_qkv: float32 [3, 768, 768], P(None, None, 'tensor')
- grad_b_qv: float32 [2, 768], P(None, 'tensor')
- grad_w_out: float32 [768, 768], P('tensor')
- grad_b_out: float32 [768], replicated
- grad_ln1_gain: float32 [768], replicated
- grad_ln1_bias: float32 [768], replicated
- grad_w_up: float32 [768, 3072], P(None, 'tensor')
- grad_b_up: float32 [3072], P('tensor')
- grad_w_down: float32 [3072, 768], P('tensor')
- grad_b_down: float32 [768], replicated
- grad_ln2_gain: float32 [768], replicated
- grad_ln2_bias: float32 [768], replicated
The draws below stay inside these ranges and needn't reach their ends.
Inputs may be any that keep to these rules, and one draw needn't show every extreme that they name: `segments`: within a sequence segment numbers never fall; each sequence holds 8 documents, the longest of half of 2048 tokens.
All inputs are finite; a program needn't handle non-finite values.
Results may differ from the reference program's by a relative error of at most 0.014.
Values may be sent and summed in bfloat16 or wider, within the bound.
No kernel may reach another device: no remote copies, remote signals or barrier semaphores. Data moves between devices by JAX's collectives and lax.ppermute only.
A program may use at most 128 MiB of HBM per device.

```python
import math
import jax
import jax.numpy as jnp
import numpy as np
from jax import lax

D = 768
H = 12
HEAD_SIZE = 64
FF = 3072
SEQ_LEN = 2048
DOCS = 8
TOKENS = 16384
N_DP = 8


def set_ends(result, own_key, smallest, high):
    spot = [jax.random.randint(jax.random.fold_in(own_key, axis), (), 0, length) for axis, length in enumerate(result.shape)]
    widest = result.shape.index(max(result.shape))
    next_to = spot[:widest] + [(spot[widest] + 1) % result.shape[widest]] + spot[widest + 1:]
    return result.at[tuple(spot)].set(smallest).at[tuple(next_to)].set(high)


def steps_of(own_key, dims, split, smallest, largest):
    level = 1.0
    for position, shards_of in split:
        steps = jax.random.uniform(jax.random.fold_in(jax.random.fold_in(own_key, 6), position), (shards_of,), jnp.float32, smallest / len(split), largest / len(split))
        level = level * jnp.repeat(jnp.exp(steps), dims[position] // shards_of).reshape((-1,) + (1,) * (len(dims) - 1 - position))
    return level


def length_profile(count, total, most, slope):
    weights = [(1 << 20) // math.isqrt(grade ** slope) + 1 for grade in range(2, count + 1)]
    rest, holding = total - most - (count - 1), [1] * (count - 1)
    while rest > 0:
        movable = [i for i in range(count - 1) if holding[i] < most]
        whole, remaining = sum([weights[i] for i in movable]), rest
        for i in movable:
            addition = min(most - holding[i], max(1, remaining * weights[i] // whole), rest)
            holding[i] = holding[i] + addition
            rest = rest - addition
    return np.array([most] + holding)


def ragged(rng, count, total, limit, skew):
    if count == 2:
        one = jax.random.randint(rng, (), max(1, total - limit), min(limit, total - 1) + 1)
        return jnp.stack([one, total - one])
    sizes = jnp.asarray(length_profile(count, total, limit, skew), jnp.int32)
    couples = (count - 1) // 2
    source_of, taker = sizes[1:1 + 2 * couples:2], sizes[2:2 + 2 * couples:2]
    slack = jnp.minimum(source_of - 1, limit - taker)
    moved = jax.random.randint(jax.random.fold_in(rng, 1), (couples,), 0, 1 << 20) % (slack + 1)
    sizes = sizes.at[1:1 + 2 * couples:2].set(source_of - moved).at[2:2 + 2 * couples:2].set(taker + moved)
    return sizes[jax.random.permutation(jax.random.fold_in(rng, 2), count)]


def scatter_about(key, extent, spread, most, pieces=(), dtype=jnp.bfloat16):
    drawn = spread * jax.random.normal(key, extent, jnp.float32)
    if pieces:
        drawn = drawn * steps_of(key, extent, pieces, -0.22, 0.18)
    return jnp.clip(drawn, -most, most).astype(dtype)


def setup_inputs(seed: int = 0) -> dict:
    seeds = jax.random.split(jax.random.key(seed), 17)
    return {
        "tokens": scatter_about(seeds[0], (TOKENS, D), 1.0, 6.0, ((0, 32),)),
        "segments": jax.vmap(lambda own: jnp.searchsorted(jnp.cumsum(ragged(own, DOCS, SEQ_LEN, SEQ_LEN // 2, 2)), jnp.arange(SEQ_LEN), side="right"))(jax.random.split(seeds[1], N_DP)).reshape((N_DP, SEQ_LEN)).astype(jnp.int32),
        "block_perm": set_ends(jax.random.randint(seeds[2], (H,), 0, 2), jax.random.fold_in(seeds[2], 1), 0, 1).astype(jnp.int32),
        "w_qkv": scatter_about(seeds[3], (3, D, D), D ** -0.5, 0.21875, ((2, 4),)),
        "b_qv": scatter_about(seeds[4], (2, D), 0.5, 3.0, ((1, 4),)),
        "w_out": scatter_about(seeds[5], (D, D), (max(1, D // 128)) ** -0.5, 2.5, ((0, 4),)),
        "b_out": scatter_about(seeds[6], (D,), 0.5, 3.0),
        "ln1_gain": jnp.clip(1.0 + 0.1 * jax.random.normal(seeds[7], (D,), jnp.float32), 0.5, 1.5).astype(jnp.bfloat16),
        "ln1_bias": scatter_about(seeds[8], (D,), 0.5, 3.0),
        "w_up": scatter_about(seeds[9], (D, FF), D ** -0.5, 0.21875, ((1, 4),)),
        "b_up": scatter_about(seeds[10], (FF,), 0.5, 3.0, ((0, 4),)),
        "w_down": scatter_about(seeds[11], (FF, D), FF ** -0.5, 0.109375, ((0, 4),)),
        "b_down": scatter_about(seeds[12], (D,), 0.5, 3.0),
        "ln2_gain": jnp.clip(1.0 + 0.1 * jax.random.normal(seeds[13], (D,), jnp.float32), 0.5, 1.5).astype(jnp.bfloat16),
        "ln2_bias": scatter_about(seeds[14], (D,), 0.5, 3.0),
        "cotangent": scatter_about(seeds[15], (TOKENS, D), 1.0, 6.0, ((0, 32),)),
    }


@jax.custom_vjp
def low(v):
    return lax.optimization_barrier(v.astype(jnp.bfloat16)).astype(jnp.float32)

@jax.custom_vjp
def lowered_pullback(v):
    return v

def low_keep(v):
    return (low(v), None)

def low_pass(kept, grad):
    return (grad,)

def back_keep(v):
    return (v, None)

def back_low(kept, grad):
    return (low(grad),)
low.defvjp(low_keep, low_pass)
lowered_pullback.defvjp(back_keep, back_low)
highest_precision = lax.Precision.HIGHEST
epsilon = 1e-05

def norm_layer(resid, gain_vec, shift_vec):
    row_mean = lax.optimization_barrier(jnp.mean(resid, axis=-1, keepdims=True))
    centered = resid - row_mean
    row_var = lax.optimization_barrier(jnp.mean(centered * centered, axis=-1, keepdims=True))
    return centered * lax.rsqrt(row_var + epsilon) * gain_vec + shift_vec

def head_attend(queries, key_rows, values, swap_flag, seg_row):
    half_len = queries.shape[0] // 2
    query_block_rows = queries.reshape(2, half_len, -1)
    key_block_rows = key_rows.reshape(2, half_len, -1)
    value_block_rows = values.reshape(2, half_len, -1)
    seg_blocks = seg_row.reshape(2, half_len)
    flipped = swap_flag == 1
    key_block_rows = jnp.where(flipped, key_block_rows[::-1], key_block_rows)
    value_block_rows = jnp.where(flipped, value_block_rows[::-1], value_block_rows)
    seg_keys = jnp.where(flipped, seg_blocks[::-1], seg_blocks)
    allowed = seg_blocks[:, :, None] == seg_keys[:, None, :]
    score_matrix = lowered_pullback(jnp.einsum('gti,gri->gtr', query_block_rows, key_block_rows, precision=highest_precision) * HEAD_SIZE ** (-0.5))
    row_max = jnp.maximum(lax.optimization_barrier(jnp.max(jnp.where(allowed, score_matrix, -1e+30), axis=-1)), 0.0)
    raised = jnp.where(allowed, jnp.exp(jnp.where(allowed, score_matrix, 0.0) - row_max[..., None]), 0.0)
    denominator = jnp.exp(-row_max) + lax.optimization_barrier(jnp.sum(raised, axis=-1))
    attention_probability = low(raised / denominator[..., None])
    context_output = jnp.einsum('lyz,lzt->lyt', attention_probability, value_block_rows, precision=highest_precision)
    return context_output.reshape(2 * half_len, -1)

def layer(params, inputs, seg_row, block_perm):
    w_qkv, b_qv, w_out, b_out, ln1_gain, ln1_bias, w_up, b_up, w_down, b_down, ln2_gain, ln2_bias = params
    projected = jnp.einsum('sd,cde->cse', inputs, w_qkv, precision=highest_precision)
    queries = lowered_pullback(low(projected[0] + b_qv[0]))
    key_rows = lowered_pullback(low(projected[1]))
    values = lowered_pullback(low(projected[2] + b_qv[1]))

    def split_heads(matrix):
        return matrix.reshape(SEQ_LEN, H, HEAD_SIZE).transpose(1, 0, 2)

    def attend_item(packed):
        return head_attend(packed[0], packed[1], packed[2], packed[3], seg_row)
    heads_out = lax.map(jax.checkpoint(attend_item), (split_heads(queries), split_heads(key_rows), split_heads(values), block_perm))
    context_output = lowered_pullback(low(heads_out.transpose(1, 0, 2).reshape(SEQ_LEN, D)))
    attended = lowered_pullback(jnp.dot(context_output, w_out, precision=highest_precision) + b_out)
    normed_one = norm_layer(inputs + attended, ln1_gain, ln1_bias)
    pre_act = lowered_pullback(jnp.dot(low(normed_one), w_up, precision=highest_precision) + b_up)
    act_low = low(jax.nn.gelu(pre_act, approximate=False))
    ffn_out = lowered_pullback(jnp.dot(act_low, w_down, precision=highest_precision) + b_down)
    return norm_layer(normed_one + ffn_out, ln2_gain, ln2_bias)

def reference(tokens, segments, block_perm, w_qkv, b_qv, w_out, b_out, ln1_gain, ln1_bias, w_up, b_up, w_down, b_down, ln2_gain, ln2_bias, cotangent):
    params = tuple((weight.astype(jnp.float32) for weight in (w_qkv, b_qv, w_out, b_out, ln1_gain, ln1_bias, w_up, b_up, w_down, b_down, ln2_gain, ln2_bias)))
    inputs_all = tokens.astype(jnp.float32).reshape(N_DP, SEQ_LEN, D)
    cotangents = cotangent.astype(jnp.float32).reshape(N_DP, SEQ_LEN, D)

    def advance(totals, slices):
        inputs, seq_cot, seg_row = slices

        def forward(weights_in, inputs_in):
            return layer(weights_in, inputs_in, seg_row, block_perm)
        outputs, pullback = jax.vjp(forward, params, inputs)
        grad_params, grad_inputs = pullback(seq_cot)
        totals = jax.tree.map(jnp.add, totals, grad_params)
        return (totals, (outputs.astype(jnp.bfloat16), grad_inputs.astype(jnp.bfloat16)))
    zeros_init = jax.tree.map(jnp.zeros_like, params)
    totals, (outputs, grad_inputs) = lax.scan(advance, zeros_init, (inputs_all, cotangents, segments))
    return (outputs.reshape(N_DP * SEQ_LEN, D), grad_inputs.reshape(N_DP * SEQ_LEN, D), totals[0], totals[1], totals[2], totals[3], totals[4], totals[5], totals[6], totals[7], totals[8], totals[9], totals[10], totals[11])
```

```python
import jax
import jax.numpy as jnp
from jax import lax
from jax.sharding import PartitionSpec as P

HEAD_SIZE = 64


epsilon = 1e-05


def norm_layer(resid, gain_vec, shift_vec):
    row_mean = jnp.mean(resid, axis=-1, keepdims=True)
    centered = resid - row_mean
    row_var = jnp.mean(centered * centered, axis=-1, keepdims=True)
    return centered * lax.rsqrt(row_var + epsilon) * gain_vec + shift_vec


def gelu_exact(pre_act):
    return jax.nn.gelu(pre_act, approximate=False)


def blocks_of(matrix, heads_local):
    seq_len = matrix.shape[0]
    head_dim = matrix.shape[1] // heads_local
    return (
        matrix.reshape(seq_len, heads_local, head_dim)
        .transpose(1, 0, 2)
        .reshape(heads_local * 2, seq_len // 2, head_dim)
    )


def rows_of(blocks, heads_local):
    half_len = blocks.shape[1]
    head_dim = blocks.shape[2]
    return (
        blocks.reshape(heads_local, half_len * 2, head_dim)
        .transpose(1, 0, 2)
        .reshape(half_len * 2, heads_local * head_dim)
    )


def swap_blocks(blocks, block_perm):
    heads_local = block_perm.shape[0]
    shaped = blocks.reshape((heads_local, 2) + blocks.shape[1:])
    flag_mask = (block_perm == 1).reshape((heads_local,) + (1,) * blocks.ndim)
    return jnp.where(flag_mask, shaped[:, ::-1], shaped).reshape(blocks.shape)


def block_scores(query_blk, key_blk, seg_query, seg_key):
    allowed = seg_query[:, None] == seg_key[None, :]
    score_matrix = jnp.einsum(
        "qd,kd->qk", query_blk, key_blk, preferred_element_type=jnp.float32
    ) * HEAD_SIZE ** (-0.5)
    raised_base = jnp.where(allowed, score_matrix, 0.0)
    return (allowed, score_matrix, raised_base)


def attend_block(packed):
    query_blk, key_blk, value_blk, seg_query, seg_key = packed
    allowed, score_matrix, raised_base = block_scores(query_blk, key_blk, seg_query, seg_key)
    row_max = jnp.maximum(jnp.max(jnp.where(allowed, score_matrix, -1e30), axis=1), 0.0)
    raised = jnp.where(allowed, jnp.exp(raised_base - row_max[:, None]), 0.0)
    denominator = jnp.exp(-row_max) + jnp.sum(raised, axis=1)
    attention_probability = raised / denominator[:, None]
    context_output = jnp.dot(
        attention_probability.astype(jnp.bfloat16), value_blk, preferred_element_type=jnp.float32
    )
    return (context_output.astype(jnp.bfloat16), row_max, denominator)


def attend_back(packed):
    query_blk, key_blk, value_blk, seg_query, seg_key, row_max, denominator, grad_ctx = packed
    allowed, score_matrix, raised_base = block_scores(query_blk, key_blk, seg_query, seg_key)
    raised = jnp.where(allowed, jnp.exp(raised_base - row_max[:, None]), 0.0)
    attention_probability = raised / denominator[:, None]
    grad_prob = jnp.einsum("qd,kd->qk", grad_ctx, value_blk, preferred_element_type=jnp.float32)
    delta_rows = jnp.sum(attention_probability * grad_prob, axis=1)
    grad_scores = (attention_probability * (grad_prob - delta_rows[:, None])).astype(jnp.bfloat16)
    scale_factor = HEAD_SIZE ** (-0.5)
    grad_query = jnp.dot(grad_scores, key_blk, preferred_element_type=jnp.float32) * scale_factor
    grad_key = (
        jnp.einsum("qk,qd->kd", grad_scores, query_blk, preferred_element_type=jnp.float32)
        * scale_factor
    )
    grad_value = jnp.einsum(
        "qk,qd->kd",
        attention_probability.astype(jnp.bfloat16),
        grad_ctx,
        preferred_element_type=jnp.float32,
    )
    return (grad_query, grad_key, grad_value)


def body(
    tokens,
    segments,
    block_perm,
    w_qkv,
    b_qv,
    w_out,
    b_out,
    ln1_gain,
    ln1_bias,
    w_up,
    b_up,
    w_down,
    b_down,
    ln2_gain,
    ln2_bias,
    cotangent,
):
    heads_local = block_perm.shape[0]
    width = tokens.shape[1]
    tensor_count = lax.axis_size("tensor")
    gathered = lax.all_gather(tokens, "tensor", axis=0, tiled=True)
    seq_len = gathered.shape[0]
    projected = jnp.einsum("sd,cde->cse", gathered, w_qkv, preferred_element_type=jnp.float32)
    bias_qv = b_qv.astype(jnp.float32)
    queries = (projected[0] + bias_qv[0]).astype(jnp.bfloat16)
    key_rows = projected[1].astype(jnp.bfloat16)
    values = (projected[2] + bias_qv[1]).astype(jnp.bfloat16)
    query_block_rows = blocks_of(queries, heads_local)
    key_block_rows = swap_blocks(blocks_of(key_rows, heads_local), block_perm)
    value_block_rows = swap_blocks(blocks_of(values, heads_local), block_perm)
    seg_query = jnp.tile(segments[0].reshape(2, seq_len // 2), (heads_local, 1))
    seg_key = swap_blocks(seg_query, block_perm)
    context_output, row_max, denominator = lax.map(
        attend_block, (query_block_rows, key_block_rows, value_block_rows, seg_query, seg_key)
    )
    context_rows = rows_of(context_output, heads_local)
    attended = lax.psum_scatter(
        jnp.dot(context_rows, w_out, preferred_element_type=jnp.bfloat16),
        "tensor",
        scatter_dimension=0,
        tiled=True,
    )
    resid_one = tokens.astype(jnp.float32) + (attended + b_out.astype(jnp.float32))
    normed_one, ln1_pull = jax.vjp(
        norm_layer, resid_one, ln1_gain.astype(jnp.float32), ln1_bias.astype(jnp.float32)
    )
    hidden_in = lax.all_gather(normed_one.astype(jnp.bfloat16), "tensor", axis=0, tiled=True)
    pre_act = jnp.dot(hidden_in, w_up, preferred_element_type=jnp.float32) + b_up.astype(
        jnp.float32
    )
    activated, gelu_pull = jax.vjp(gelu_exact, pre_act)
    act_low = activated.astype(jnp.bfloat16)
    ffn_out = lax.psum_scatter(
        jnp.dot(act_low, w_down, preferred_element_type=jnp.bfloat16),
        "tensor",
        scatter_dimension=0,
        tiled=True,
    ) + b_down.astype(jnp.float32)
    resid_two = normed_one + ffn_out
    output, ln2_pull = jax.vjp(
        norm_layer, resid_two, ln2_gain.astype(jnp.float32), ln2_bias.astype(jnp.float32)
    )
    grad_resid_two, grad_ln2_gain, grad_ln2_bias = ln2_pull(cotangent.astype(jnp.float32))
    grad_ffn_rows = lax.all_gather(
        grad_resid_two.astype(jnp.bfloat16), "tensor", axis=0, tiled=True
    )
    grad_b_down = jnp.sum(grad_ffn_rows, axis=0, dtype=jnp.float32)
    grad_w_down = jnp.einsum(
        "sf,sd->fd", act_low, grad_ffn_rows, preferred_element_type=jnp.float32
    )
    grad_act = jnp.einsum("sd,fd->sf", grad_ffn_rows, w_down, preferred_element_type=jnp.float32)
    (grad_pre,) = gelu_pull(grad_act)
    grad_pre_low = grad_pre.astype(jnp.bfloat16)
    grad_b_up = jnp.sum(grad_pre_low, axis=0, dtype=jnp.float32)
    grad_w_up = jnp.einsum("sd,sf->df", hidden_in, grad_pre_low, preferred_element_type=jnp.float32)
    grad_normed = grad_resid_two + lax.psum_scatter(
        jnp.einsum("sf,df->sd", grad_pre_low, w_up, preferred_element_type=jnp.bfloat16),
        "tensor",
        scatter_dimension=0,
        tiled=True,
    )
    grad_resid_one, grad_ln1_gain, grad_ln1_bias = ln1_pull(grad_normed)
    grad_attn_rows = lax.all_gather(
        grad_resid_one.astype(jnp.bfloat16), "tensor", axis=0, tiled=True
    )
    grad_b_out = jnp.sum(grad_attn_rows, axis=0, dtype=jnp.float32)
    grad_w_out = jnp.einsum(
        "se,sd->ed", context_rows, grad_attn_rows, preferred_element_type=jnp.float32
    )
    grad_context = jnp.einsum(
        "sd,ed->se", grad_attn_rows, w_out, preferred_element_type=jnp.float32
    ).astype(jnp.bfloat16)
    grad_ctx_blocks = blocks_of(grad_context, heads_local)
    grad_query, grad_key, grad_value = lax.map(
        attend_back,
        (
            query_block_rows,
            key_block_rows,
            value_block_rows,
            seg_query,
            seg_key,
            row_max,
            denominator,
            grad_ctx_blocks,
        ),
    )
    grad_key = swap_blocks(grad_key, block_perm)
    grad_value = swap_blocks(grad_value, block_perm)
    grad_proj = jnp.stack(
        [
            rows_of(grad_query, heads_local),
            rows_of(grad_key, heads_local),
            rows_of(grad_value, heads_local),
        ]
    ).astype(jnp.bfloat16)
    grad_b_qv = jnp.stack(
        [
            jnp.sum(grad_proj[0], axis=0, dtype=jnp.float32),
            jnp.sum(grad_proj[2], axis=0, dtype=jnp.float32),
        ]
    )
    grad_w_qkv = jnp.einsum("sd,cse->cde", gathered, grad_proj, preferred_element_type=jnp.float32)
    grad_in_part = jnp.einsum("cse,cde->sd", grad_proj, w_qkv, preferred_element_type=jnp.bfloat16)
    norm_grads = jnp.stack([grad_ln1_gain, grad_ln1_bias, grad_ln2_gain, grad_ln2_bias])
    norm_tiled = jnp.broadcast_to(norm_grads[None], (tensor_count, 4, width))
    grad_in_local, norm_summed = (
        lax.psum_scatter(grad_in_part, "tensor", scatter_dimension=0, tiled=True),
        lax.psum_scatter(norm_tiled, "tensor", scatter_dimension=0, tiled=True),
    )
    grad_tokens = (grad_resid_one + grad_in_local).astype(jnp.bfloat16)
    norm_summed = norm_summed[0]
    grad_w_qkv, grad_w_out, grad_w_up, grad_w_down = (
        lax.psum(v.astype(jnp.bfloat16), "dp").astype(jnp.float32)
        for v in (grad_w_qkv, grad_w_out, grad_w_up, grad_w_down)
    )
    (grad_b_qv, grad_b_out, norm_summed, grad_b_up, grad_b_down) = lax.psum(
        (grad_b_qv, grad_b_out, norm_summed, grad_b_up, grad_b_down), "dp"
    )
    return (
        output.astype(jnp.bfloat16),
        grad_tokens,
        grad_w_qkv,
        grad_b_qv,
        grad_w_out,
        grad_b_out,
        norm_summed[0],
        norm_summed[1],
        grad_w_up,
        grad_b_up,
        grad_w_down,
        grad_b_down,
        norm_summed[2],
        norm_summed[3],
    )


def solution(mesh):
    placed = (
        P(("dp", "tensor"), None),
        P("dp", None),
        P("tensor"),
        P(None, None, "tensor"),
        P(None, "tensor"),
        P("tensor", None),
        P(),
        P(),
        P(),
        P(None, "tensor"),
        P("tensor"),
        P("tensor", None),
        P(),
        P(),
        P(),
        P(("dp", "tensor"), None),
    )
    return jax.shard_map(
        body,
        mesh=mesh,
        in_specs=placed,
        out_specs=(
            P(("dp", "tensor"), None),
            P(("dp", "tensor"), None),
            P(None, None, "tensor"),
            P(None, "tensor"),
            P("tensor", None),
            P(),
            P(),
            P(),
            P(None, "tensor"),
            P("tensor"),
            P("tensor", None),
            P(),
            P(),
            P(),
        ),
        check_vma=False,
    )
```

```python
import jax
import jax.numpy as jnp
from jax import lax
from jax.experimental import pallas as pl
from jax.experimental.pallas import tpu as pltpu
from jax.sharding import PartitionSpec as P

HEAD_SIZE = 64
SCALE = HEAD_SIZE ** (-0.5)
EPSILON = 1e-05
NEG = -1e30
TQ = 256
TK = 512
F32 = jnp.float32
BF16 = jnp.bfloat16


def dot_nt(a, b):
    return lax.dot_general(a, b, (((1,), (1,)), ((), ())), preferred_element_type=F32)


def dot_tn(a, b):
    return lax.dot_general(a, b, (((0,), (0,)), ((), ())), preferred_element_type=F32)


def dot_nn(a, b):
    return lax.dot_general(a, b, (((1,), (0,)), ((), ())), preferred_element_type=F32)


def head_mask(rows, cols, head):
    lane = lax.broadcasted_iota(jnp.int32, (rows, cols), 1)
    return (lane >= head * HEAD_SIZE) & (lane < (head + 1) * HEAD_SIZE)


def attend_kernel(perm_ref, meet_ref, q_ref, k_ref, v_ref, segc_ref, segr_ref, ctx_ref, lse_ref, m_s, l_s, acc_s):
    heads = perm_ref.shape[0]
    seq, cols = q_ref.shape
    q_tiles = seq // TQ
    half_q = q_tiles // 2
    half_k = seq // TK // 2

    def tile(i, carry):
        row0 = pl.multiple_of(i * TQ, TQ)
        block = i // half_q
        q_all = q_ref[pl.ds(row0, TQ), :].astype(F32) * SCALE
        seg_q = segc_ref[pl.ds(row0, TQ), 0:1]
        out = jnp.zeros((TQ, cols), F32)
        for h in range(heads):
            mask = head_mask(TQ, cols, h)
            q_h = jnp.where(mask, q_all, 0.0).astype(BF16)
            key_block = jnp.where(perm_ref[h] == 1, 1 - block, block)
            m_s[...] = jnp.zeros_like(m_s)
            l_s[...] = jnp.ones_like(l_s)
            acc_s[...] = jnp.zeros_like(acc_s)
            for j in range(half_k):
                kt = key_block * half_k + j

                @pl.when(meet_ref[i, kt] == 1)
                def _():
                    key0 = pl.multiple_of(kt * TK, TK)
                    seg_k = segr_ref[pl.ds(kt, 1), :]
                    s = dot_nt(q_h, k_ref[pl.ds(key0, TK), :])
                    s = jnp.where(seg_q == seg_k, s, NEG)
                    m_old = m_s[:, 0:1]
                    m_new = jnp.maximum(m_old, jnp.max(s, axis=1, keepdims=True))
                    alpha = jnp.exp(m_old - m_new)
                    p = jnp.exp(s - m_new)
                    l_new = alpha * l_s[:, 0:1] + jnp.sum(p, axis=1, keepdims=True)
                    acc_s[...] = alpha * acc_s[...] + dot_nn(p.astype(BF16), v_ref[pl.ds(key0, TK), :])
                    m_s[...] = jnp.broadcast_to(m_new, m_s.shape)
                    l_s[...] = jnp.broadcast_to(l_new, l_s.shape)

            out = jnp.where(mask, acc_s[...] / l_s[:, 0:1], out)
            stat = jnp.transpose(m_s[...] + jnp.log(l_s[...]))
            lse_ref[i, h : h + 1, :] = stat[0:1, :]
        ctx_ref[pl.ds(row0, TQ), :] = out.astype(BF16)
        return carry

    lax.fori_loop(0, q_tiles, tile, 0)


def attend_back_kernel(
    perm_ref, meet_ref, q_ref, k_ref, v_ref, g_ref, ctx_ref, segc_ref, segr_ref, lse_ref,
    dq_ref, dk_ref, dv_ref, dq_s, dk_s, dv_s,
):
    heads = perm_ref.shape[0]
    seq, cols = q_ref.shape
    q_tiles = seq // TQ
    half_q = q_tiles // 2
    half_k = seq // TK // 2
    dk_s[...] = jnp.zeros_like(dk_s)
    dv_s[...] = jnp.zeros_like(dv_s)

    def tile(i, carry):
        row0 = pl.multiple_of(i * TQ, TQ)
        block = i // half_q
        q_all = q_ref[pl.ds(row0, TQ), :].astype(F32) * SCALE
        g_all = g_ref[pl.ds(row0, TQ), :]
        gc = g_all.astype(F32) * ctx_ref[pl.ds(row0, TQ), :].astype(F32)
        gc_t = jnp.transpose(gc)
        seg_q = segr_ref[pl.ds(i // (TK // TQ), 1), :]
        seg_q = jnp.where(i % 2 == 0, seg_q[:, :TQ], seg_q[:, TQ:])
        out = jnp.zeros((TQ, cols), F32)
        for h in range(heads):
            mask = head_mask(TQ, cols, h)
            q_h = jnp.where(mask, q_all, 0.0).astype(BF16)
            g_h = jnp.where(mask, g_all, jnp.zeros_like(g_all))
            delta = jnp.sum(gc_t[h * HEAD_SIZE : (h + 1) * HEAD_SIZE, :], axis=0, keepdims=True)
            lse = lse_ref[i, h : h + 1, :]
            key_block = jnp.where(perm_ref[h] == 1, 1 - block, block)
            dq_s[...] = jnp.zeros_like(dq_s)
            for j in range(half_k):
                kt = key_block * half_k + j

                @pl.when(meet_ref[i, kt] == 1)
                def _():
                    key0 = pl.multiple_of(kt * TK, TK)
                    keys = k_ref[pl.ds(key0, TK), :]
                    seg_k = segc_ref[pl.ds(key0, TK), 0:1]
                    s = dot_nt(keys, q_h)
                    p = jnp.exp(jnp.where(seg_k == seg_q, s - lse, NEG))
                    dp = dot_nt(v_ref[pl.ds(key0, TK), :], g_h)
                    ds = (p * (dp - delta)).astype(BF16)
                    dv_s[pl.ds(key0, TK), :] += dot_nn(p.astype(BF16), g_h)
                    dk_s[pl.ds(key0, TK), :] += dot_nn(ds, q_h)
                    dq_s[...] += dot_tn(ds, keys)

            out = jnp.where(mask, dq_s[...], out)
        dq_ref[pl.ds(row0, TQ), :] = (out * SCALE).astype(BF16)
        return carry

    lax.fori_loop(0, q_tiles, tile, 0)
    dk_ref[...] = dk_s[...].astype(BF16)
    dv_ref[...] = dv_s[...].astype(BF16)


def vmem_spec():
    return pl.BlockSpec(memory_space=pltpu.VMEM)


def smem_spec():
    return pl.BlockSpec(memory_space=pltpu.SMEM)


def attend(perm, meet, q, k, v, segc, segr):
    seq, cols = q.shape
    return pl.pallas_call(
        attend_kernel,
        in_specs=[smem_spec(), smem_spec()] + [vmem_spec()] * 5,
        out_specs=[vmem_spec()] * 2,
        out_shape=[
            jax.ShapeDtypeStruct((seq, cols), BF16),
            jax.ShapeDtypeStruct((seq // TQ, 8, TQ), F32),
        ],
        scratch_shapes=[pltpu.VMEM((TQ, 128), F32), pltpu.VMEM((TQ, 128), F32), pltpu.VMEM((TQ, cols), F32)],
        name="attend",
    )(perm, meet, q, k, v, segc, segr)


def attend_back(perm, meet, q, k, v, g, ctx, segc, segr, lse):
    seq, cols = q.shape
    return pl.pallas_call(
        attend_back_kernel,
        in_specs=[smem_spec(), smem_spec()] + [vmem_spec()] * 8,
        out_specs=[vmem_spec()] * 3,
        out_shape=[jax.ShapeDtypeStruct((seq, cols), BF16)] * 3,
        scratch_shapes=[pltpu.VMEM((TQ, cols), F32), pltpu.VMEM((seq, cols), F32), pltpu.VMEM((seq, cols), F32)],
        name="attend_back",
    )(perm, meet, q, k, v, g, ctx, segc, segr, lse)


def norm_parts(resid):
    centered = resid - jnp.mean(resid, axis=-1, keepdims=True)
    rstd = lax.rsqrt(jnp.mean(centered * centered, axis=-1, keepdims=True) + EPSILON)
    return centered * rstd, rstd


def norm_back(cot, normal, rstd, gain):
    dn = cot * gain
    return rstd * (
        dn - jnp.mean(dn, axis=-1, keepdims=True) - normal * jnp.mean(dn * normal, axis=-1, keepdims=True)
    )


def body(
    tokens,
    segments,
    block_perm,
    w_qkv,
    b_qv,
    w_out,
    b_out,
    ln1_gain,
    ln1_bias,
    w_up,
    b_up,
    w_down,
    b_down,
    ln2_gain,
    ln2_bias,
    cotangent,
):
    count = lax.axis_size("tensor")
    place = lax.axis_index("tensor")
    rows, width = tokens.shape
    cols = w_out.shape[0]
    units = w_up.shape[1]

    def swap(value, mask):
        return lax.ppermute(value, "tensor", [(i, i ^ mask) for i in range(count)])

    def after(value, *others):
        return lax.optimization_barrier((value,) + others)[0]

    x2 = swap(tokens, 2)
    x1 = swap(tokens, 1)
    x3 = swap(x2, 1)
    x_all = jnp.concatenate([tokens, x1, x2, x3], axis=0)
    seq = x_all.shape[0]

    packed_a = jnp.concatenate([w_out, w_up, jnp.broadcast_to(b_up[None], (16, units))], axis=0)
    packed_a = after(packed_a, x2)
    pa2 = swap(packed_a, 2)
    pa1 = swap(packed_a, 1)
    pa3 = swap(pa2, 1)
    wd_src = after(w_down, pa2)
    wd2 = swap(wd_src, 2)
    wd1 = swap(wd_src, 1)
    wd3 = swap(wd2, 1)
    parts_a = [packed_a, pa1, pa2, pa3]
    wo = [p[:cols] for p in parts_a]
    wu = [p[cols : cols + width] for p in parts_a]
    bu = [p[cols + width].astype(F32) for p in parts_a]
    wd = [w_down, wd1, wd2, wd3]

    seg4 = segments[0].reshape(count, rows)
    seg_row = jnp.concatenate(
        [lax.dynamic_slice_in_dim(seg4, place ^ m, 1, 0) for m in range(count)], axis=0
    ).reshape(seq)
    segc = jnp.broadcast_to(seg_row[:, None], (seq, 128))
    segr = seg_row.reshape(seq // TK, TK)
    q_lo, q_hi = (f(seg_row.reshape(seq // TQ, TQ), axis=1) for f in (jnp.min, jnp.max))
    k_lo, k_hi = (f(segr, axis=1) for f in (jnp.min, jnp.max))
    meet = ((q_lo[:, None] <= k_hi[None]) & (k_lo[None] <= q_hi[:, None])).astype(jnp.int32)

    bias_qv = b_qv.astype(F32)
    q = (dot_nn(x_all, w_qkv[0]) + bias_qv[0]).astype(BF16)
    k = dot_nn(x_all, w_qkv[1]).astype(BF16)
    v = (dot_nn(x_all, w_qkv[2]) + bias_qv[1]).astype(BF16)
    ctx, lse = attend(block_perm, meet, q, k, v, segc, segr)

    ctx_own = [ctx[:rows]] + [swap(ctx[m * rows : (m + 1) * rows], m) for m in range(1, count)]
    x32 = tokens.astype(F32)
    attended = sum(dot_nn(c, w) for c, w in zip(ctx_own, wo)) + b_out.astype(F32)
    gain1, gain2 = ln1_gain.astype(F32), ln2_gain.astype(F32)
    normal1, rstd1 = norm_parts(x32 + attended)
    normed_one = normal1 * gain1 + ln1_bias.astype(F32)
    hidden = normed_one.astype(BF16)

    acts, slopes = [], []
    for m in range(count):
        pre = dot_nn(hidden, wu[m]) + bu[m]
        cdf = 0.5 * (1.0 + lax.erf(pre * (2.0 ** -0.5)))
        pdf = jnp.exp(-0.5 * pre * pre) * (0.5 / jnp.pi) ** 0.5
        acts.append((pre * cdf).astype(BF16))
        slopes.append(cdf + pre * pdf)
    ffn = sum(dot_nn(a, w) for a, w in zip(acts, wd)) + b_down.astype(F32)
    normal2, rstd2 = norm_parts(normed_one + ffn)
    output = (normal2 * gain2 + ln2_bias.astype(F32)).astype(BF16)

    cot = cotangent.astype(F32)
    g_two = norm_back(cot, normal2, rstd2, gain2)
    g_two_low = g_two.astype(BF16)
    d_ln2_gain = jnp.sum(cot * normal2, axis=0)
    d_ln2_bias = jnp.sum(cot, axis=0)
    d_b_down = jnp.sum(g_two_low.astype(F32), axis=0)

    def scatter_parts(parts):
        sent = swap(jnp.concatenate([parts[1], parts[3]], axis=0), 1)
        size = parts[0].shape[0]
        far = (parts[2].astype(F32) + sent[size:].astype(F32)).astype(BF16)
        return (parts[0].astype(F32) + sent[:size].astype(F32)) + swap(far, 2).astype(F32)

    d_wd = scatter_parts([dot_tn(a, g_two_low).astype(BF16) for a in acts])
    g_pre = [(dot_nt(g_two_low, w) * s).astype(BF16) for w, s in zip(wd, slopes)]
    d_wu_parts = []
    for m in range(count):
        d_bu = jnp.sum(g_pre[m].astype(F32), axis=0)
        d_wu_parts.append(
            jnp.concatenate(
                [dot_tn(hidden, g_pre[m]).astype(BF16), jnp.broadcast_to(d_bu[None], (16, units)).astype(BF16)], axis=0
            )
        )
    d_wu = scatter_parts(d_wu_parts)
    g_normed = g_two + sum(dot_nt(g, w) for g, w in zip(g_pre, wu))
    g_one = norm_back(g_normed, normal1, rstd1, gain1)
    d_ln1_gain = jnp.sum(g_normed * normal1, axis=0)
    d_ln1_bias = jnp.sum(g_normed, axis=0)
    g_one_low = g_one.astype(BF16)
    d_b_out = jnp.sum(g_one_low.astype(F32), axis=0)
    g_ctx_parts = [dot_nt(g_one_low, w).astype(BF16) for w in wo]
    g_ctx = jnp.concatenate(
        [g_ctx_parts[0]] + [swap(g_ctx_parts[m], m) for m in range(1, count)], axis=0
    )
    d_wo = scatter_parts([dot_tn(c, g_one_low).astype(BF16) for c in ctx_own])
    small = jnp.stack([d_b_out, d_ln1_gain, d_ln1_bias, d_b_down, d_ln2_gain, d_ln2_bias, d_b_out, d_b_out])
    small = small + swap(small, 1)
    small = small + swap(small, 2)

    dq, dk, dv = attend_back(block_perm, meet, q, k, v, g_ctx, ctx, segc, segr, lse)
    part = dot_nt(dq, w_qkv[0]) + dot_nt(dk, w_qkv[1]) + dot_nt(dv, w_qkv[2])
    part = part.astype(BF16)
    g_in = scatter_parts([part[m * rows : (m + 1) * rows] for m in range(count)])
    grad_tokens = (g_one + g_in).astype(BF16)
    d_qkv = jnp.stack([dot_tn(x_all, d).astype(BF16) for d in (dq, dk, dv)])
    d_bqv = jnp.stack([jnp.sum(d.astype(F32), axis=0) for d in (dq, dv)])

    d_wd, d_wu, d_wo, small = lax.psum(
        (d_wd.astype(BF16), d_wu.astype(BF16), d_wo.astype(BF16), small.astype(BF16)), "dp"
    )
    d_qkv, d_bqv = lax.psum((d_qkv, d_bqv.astype(BF16)), "dp")
    d_wd, d_wu, d_wo, small, d_qkv, d_bqv = (z.astype(F32) for z in (d_wd, d_wu, d_wo, small, d_qkv, d_bqv))
    return (
        output,
        grad_tokens,
        d_qkv,
        d_bqv,
        d_wo,
        small[0],
        small[1],
        small[2],
        d_wu[:width],
        d_wu[width],
        d_wd,
        small[3],
        small[4],
        small[5],
    )


def solution(mesh):
    placed = (
        P(("dp", "tensor"), None),
        P("dp", None),
        P("tensor"),
        P(None, None, "tensor"),
        P(None, "tensor"),
        P("tensor", None),
        P(),
        P(),
        P(),
        P(None, "tensor"),
        P("tensor"),
        P("tensor", None),
        P(),
        P(),
        P(),
        P(("dp", "tensor"), None),
    )
    return jax.shard_map(
        body,
        mesh=mesh,
        in_specs=placed,
        out_specs=(
            P(("dp", "tensor"), None),
            P(("dp", "tensor"), None),
            P(None, None, "tensor"),
            P(None, "tensor"),
            P("tensor", None),
            P(),
            P(),
            P(),
            P(None, "tensor"),
            P("tensor"),
            P("tensor", None),
            P(),
            P(),
            P(),
        ),
        check_vma=False,
    )
```

```python
import jax
import jax.numpy as jnp
from jax import lax
from jax.experimental import pallas as pl
from jax.experimental.pallas import tpu as pltpu
from jax.sharding import PartitionSpec as P

HEAD_SIZE = 64
SCALE = HEAD_SIZE ** (-0.5)
EPSILON = 1e-05
NEG = -1e30
TQ = 256
TK = 512
F32 = jnp.float32
BF16 = jnp.bfloat16


def dot_nt(a, b):
    return lax.dot_general(a, b, (((1,), (1,)), ((), ())), preferred_element_type=F32)


def dot_tn(a, b):
    return lax.dot_general(a, b, (((0,), (0,)), ((), ())), preferred_element_type=F32)


def dot_nn(a, b):
    return lax.dot_general(a, b, (((1,), (0,)), ((), ())), preferred_element_type=F32)


def head_mask(rows, cols, head):
    lane = lax.broadcasted_iota(jnp.int32, (rows, cols), 1)
    return (lane >= head * HEAD_SIZE) & (lane < (head + 1) * HEAD_SIZE)


def attend_kernel(perm_ref, meet_ref, q_ref, k_ref, v_ref, segc_ref, segr_ref, ctx_ref, lse_ref, m_s, l_s, acc_s):
    heads = perm_ref.shape[0]
    seq, cols = q_ref.shape
    q_tiles = seq // TQ
    half_q = q_tiles // 2
    half_k = seq // TK // 2

    def tile(i, carry):
        row0 = pl.multiple_of(i * TQ, TQ)
        block = i // half_q
        q_all = q_ref[pl.ds(row0, TQ), :].astype(F32) * SCALE
        seg_q = segr_ref[pl.ds(i // (TK // TQ), 1), :]
        seg_q = jnp.where(i % 2 == 0, seg_q[:, :TQ], seg_q[:, TQ:])
        m_s[...] = jnp.zeros_like(m_s)
        l_s[...] = jnp.ones_like(l_s)
        acc_s[...] = jnp.zeros_like(acc_s)
        for h in range(heads):
            here = slice(h * HEAD_SIZE, (h + 1) * HEAD_SIZE)
            q_h = jnp.where(head_mask(TQ, cols, h), q_all, 0.0).astype(BF16)
            key_block = jnp.where(perm_ref[h] == 1, 1 - block, block)
            for j in range(half_k):
                kt = key_block * half_k + j

                @pl.when(meet_ref[i, kt] == 1)
                def _():
                    key0 = pl.multiple_of(kt * TK, TK)
                    seg_k = segc_ref[pl.ds(key0, TK), 0:1]
                    s = dot_nt(k_ref[pl.ds(key0, TK), :], q_h)
                    s = jnp.where(seg_k == seg_q, s, NEG)
                    m_old = m_s[h : h + 1, :]
                    m_new = jnp.maximum(m_old, jnp.max(s, axis=0, keepdims=True))
                    alpha = jnp.exp(m_old - m_new)
                    p = jnp.exp(s - m_new)
                    l_s[h : h + 1, :] = alpha * l_s[h : h + 1, :] + jnp.sum(p, axis=0, keepdims=True)
                    part = dot_tn(v_ref[pl.ds(key0, TK), :], p.astype(BF16))
                    acc_s[here, :] = alpha * acc_s[here, :] + part[here, :]
                    m_s[h : h + 1, :] = m_new

            acc_s[here, :] = acc_s[here, :] / l_s[h : h + 1, :]
        lse_ref[i] = m_s[...] + jnp.log(l_s[...])
        ctx_ref[pl.ds(row0, TQ), :] = jnp.transpose(acc_s[...]).astype(BF16)
        return carry

    lax.fori_loop(0, q_tiles, tile, 0)


def attend_back_kernel(
    perm_ref, meet_ref, q_ref, k_ref, v_ref, g_ref, ctx_ref, segc_ref, segr_ref, lse_ref,
    dq_ref, dk_ref, dv_ref, dq_s, dk_s, dv_s,
):
    heads = perm_ref.shape[0]
    seq, cols = q_ref.shape
    q_tiles = seq // TQ
    half_q = q_tiles // 2
    half_k = seq // TK // 2
    dk_s[...] = jnp.zeros_like(dk_s)
    dv_s[...] = jnp.zeros_like(dv_s)

    def tile(i, carry):
        row0 = pl.multiple_of(i * TQ, TQ)
        block = i // half_q
        q_all = q_ref[pl.ds(row0, TQ), :].astype(F32) * SCALE
        g_all = g_ref[pl.ds(row0, TQ), :]
        gc = g_all.astype(F32) * ctx_ref[pl.ds(row0, TQ), :].astype(F32)
        gc_t = jnp.transpose(gc)
        seg_q = segr_ref[pl.ds(i // (TK // TQ), 1), :]
        seg_q = jnp.where(i % 2 == 0, seg_q[:, :TQ], seg_q[:, TQ:])
        out = jnp.zeros((TQ, cols), F32)
        for h in range(heads):
            mask = head_mask(TQ, cols, h)
            q_h = jnp.where(mask, q_all, 0.0).astype(BF16)
            g_h = jnp.where(mask, g_all, jnp.zeros_like(g_all))
            delta = jnp.sum(gc_t[h * HEAD_SIZE : (h + 1) * HEAD_SIZE, :], axis=0, keepdims=True)
            lse = lse_ref[i, h : h + 1, :]
            key_block = jnp.where(perm_ref[h] == 1, 1 - block, block)
            dq_s[...] = jnp.zeros_like(dq_s)
            for j in range(half_k):
                kt = key_block * half_k + j

                @pl.when(meet_ref[i, kt] == 1)
                def _():
                    key0 = pl.multiple_of(kt * TK, TK)
                    keys = k_ref[pl.ds(key0, TK), :]
                    seg_k = segc_ref[pl.ds(key0, TK), 0:1]
                    s = dot_nt(keys, q_h)
                    p = jnp.exp(jnp.where(seg_k == seg_q, s - lse, NEG))
                    dp = dot_nt(v_ref[pl.ds(key0, TK), :], g_h)
                    ds = (p * (dp - delta)).astype(BF16)
                    dv_s[pl.ds(key0, TK), :] += dot_nn(p.astype(BF16), g_h)
                    dk_s[pl.ds(key0, TK), :] += dot_nn(ds, q_h)
                    dq_s[...] += dot_tn(ds, keys)

            out = jnp.where(mask, dq_s[...], out)
        dq_ref[pl.ds(row0, TQ), :] = (out * SCALE).astype(BF16)
        return carry

    lax.fori_loop(0, q_tiles, tile, 0)
    dk_ref[...] = dk_s[...].astype(BF16)
    dv_ref[...] = dv_s[...].astype(BF16)


def vmem_spec():
    return pl.BlockSpec(memory_space=pltpu.VMEM)


def smem_spec():
    return pl.BlockSpec(memory_space=pltpu.SMEM)


def attend(perm, meet, q, k, v, segc, segr):
    seq, cols = q.shape
    return pl.pallas_call(
        attend_kernel,
        in_specs=[smem_spec(), smem_spec()] + [vmem_spec()] * 5,
        out_specs=[vmem_spec()] * 2,
        out_shape=[
            jax.ShapeDtypeStruct((seq, cols), BF16),
            jax.ShapeDtypeStruct((seq // TQ, 8, TQ), F32),
        ],
        scratch_shapes=[pltpu.VMEM((8, TQ), F32), pltpu.VMEM((8, TQ), F32), pltpu.VMEM((cols, TQ), F32)],
        name="attend",
    )(perm, meet, q, k, v, segc, segr)


def attend_back(perm, meet, q, k, v, g, ctx, segc, segr, lse):
    seq, cols = q.shape
    return pl.pallas_call(
        attend_back_kernel,
        in_specs=[smem_spec(), smem_spec()] + [vmem_spec()] * 8,
        out_specs=[vmem_spec()] * 3,
        out_shape=[jax.ShapeDtypeStruct((seq, cols), BF16)] * 3,
        scratch_shapes=[pltpu.VMEM((TQ, cols), F32), pltpu.VMEM((seq, cols), F32), pltpu.VMEM((seq, cols), F32)],
        name="attend_back",
    )(perm, meet, q, k, v, g, ctx, segc, segr, lse)


def norm_parts(resid):
    centered = resid - jnp.mean(resid, axis=-1, keepdims=True)
    rstd = lax.rsqrt(jnp.mean(centered * centered, axis=-1, keepdims=True) + EPSILON)
    return centered * rstd, rstd


def norm_back(cot, normal, rstd, gain):
    dn = cot * gain
    return rstd * (
        dn - jnp.mean(dn, axis=-1, keepdims=True) - normal * jnp.mean(dn * normal, axis=-1, keepdims=True)
    )


def layer(
    tokens,
    segments,
    block_perm,
    w_qkv,
    b_qv,
    w_out,
    b_out,
    ln1_gain,
    ln1_bias,
    w_up,
    b_up,
    w_down,
    b_down,
    ln2_gain,
    ln2_bias,
    cotangent,
):
    count = lax.axis_size("tensor")
    place = lax.axis_index("tensor")
    group = lax.axis_size("dp")
    member = lax.axis_index("dp")
    rows, width = tokens.shape
    cols = w_out.shape[0]
    units = w_up.shape[1]

    def swap(value, mask):
        return lax.ppermute(value, "tensor", [(i, i ^ mask) for i in range(count)])

    def swap_dp(value, mask):
        return lax.ppermute(value, "dp", [(i, i ^ mask) for i in range(group)])

    def after(value, *others):
        return lax.optimization_barrier((value,) + others)[0]

    masks = [1 << i for i in range(group.bit_length() - 1)]

    def sum_dp(value):
        for mask in masks:
            half = value.shape[0] // 2
            bit = (member // mask) % 2
            sent = lax.dynamic_slice_in_dim(value, (1 - bit) * half, half, 0)
            kept = lax.dynamic_slice_in_dim(value, bit * half, half, 0)
            got = swap_dp(sent, mask)
            value = (kept.astype(F32) + got.astype(F32)).astype(BF16)
        for mask in reversed(masks):
            got = swap_dp(value, mask)
            first = (member // mask) % 2 == 0
            value = jnp.concatenate([jnp.where(first, value, got), jnp.where(first, got, value)], axis=0)
        return value

    x2 = swap(tokens, 2)
    x1 = swap(tokens, 1)
    x3 = swap(x2, 1)
    x_all = jnp.concatenate([tokens, x1, x2, x3], axis=0)
    seq = x_all.shape[0]

    slab = units // group
    wd_slab = lax.dynamic_slice_in_dim(w_down, member * slab, slab, 0)
    wd2 = lax.all_gather(swap(after(wd_slab, x2), 2), "dp", axis=0, tiled=True)
    wd1 = swap(w_down, 1)
    packed_a = jnp.concatenate([w_out, w_up, jnp.broadcast_to(b_up[None], (16, units))], axis=0)
    packed_a = after(packed_a, x2)
    pa2 = swap(packed_a, 2)
    pa1 = swap(packed_a, 1)

    seg4 = segments[0].reshape(count, rows)
    seg_row = jnp.concatenate(
        [lax.dynamic_slice_in_dim(seg4, place ^ m, 1, 0) for m in range(count)], axis=0
    ).reshape(seq)
    segc = jnp.broadcast_to(seg_row[:, None], (seq, 128))
    segr = seg_row.reshape(seq // TK, TK)
    q_lo, q_hi = (f(seg_row.reshape(seq // TQ, TQ), axis=1) for f in (jnp.min, jnp.max))
    k_lo, k_hi = (f(segr, axis=1) for f in (jnp.min, jnp.max))
    meet = ((q_lo[:, None] <= k_hi[None]) & (k_lo[None] <= q_hi[:, None])).astype(jnp.int32)

    bias_qv = b_qv.astype(F32)
    q = (dot_nn(x_all, w_qkv[0]) + bias_qv[0]).astype(BF16)
    k = dot_nn(x_all, w_qkv[1]).astype(BF16)
    v = (dot_nn(x_all, w_qkv[2]) + bias_qv[1]).astype(BF16)
    ctx, lse = attend(block_perm, meet, q, k, v, segc, segr)

    ctx_own = [ctx[:rows]] + [swap(ctx[m * rows : (m + 1) * rows], m) for m in range(1, count)]
    pa3 = swap(after(pa2, ctx), 1)
    wd3 = swap(after(wd2, ctx), 1)
    parts_a = [packed_a, pa1, pa2, pa3]
    wo = [p[:cols] for p in parts_a]
    wu = [p[cols : cols + width] for p in parts_a]
    bu = [p[cols + width].astype(F32) for p in parts_a]
    wd = [w_down, wd1, wd2, wd3]
    x32 = tokens.astype(F32)
    attended = sum(dot_nn(c, w) for c, w in zip(ctx_own, wo)) + b_out.astype(F32)
    gain1, gain2 = ln1_gain.astype(F32), ln2_gain.astype(F32)
    normal1, rstd1 = norm_parts(x32 + attended)
    normed_one = normal1 * gain1 + ln1_bias.astype(F32)
    hidden = normed_one.astype(BF16)

    acts, slopes = [], []
    for m in range(count):
        pre = dot_nn(hidden, wu[m]) + bu[m]
        cdf = 0.5 * (1.0 + lax.erf(pre * (2.0 ** -0.5)))
        pdf = jnp.exp(-0.5 * pre * pre) * (0.5 / jnp.pi) ** 0.5
        acts.append((pre * cdf).astype(BF16))
        slopes.append(cdf + pre * pdf)
    ffn = sum(dot_nn(a, w) for a, w in zip(acts, wd)) + b_down.astype(F32)
    normal2, rstd2 = norm_parts(normed_one + ffn)
    output = (normal2 * gain2 + ln2_bias.astype(F32)).astype(BF16)

    cot = cotangent.astype(F32)
    g_two = norm_back(cot, normal2, rstd2, gain2)
    g_two_low = g_two.astype(BF16)
    d_ln2_gain = jnp.sum(cot * normal2, axis=0)
    d_ln2_bias = jnp.sum(cot, axis=0)
    d_b_down = jnp.sum(g_two_low.astype(F32), axis=0)

    def to_pair(parts):
        near = swap(parts[1], 1)
        far = swap(parts[3], 1)
        return (
            (parts[0].astype(F32) + near.astype(F32)).astype(BF16),
            (parts[2].astype(F32) + far.astype(F32)).astype(BF16),
        )

    def add_far(own, far):
        return own.astype(F32) + swap(far, 2).astype(F32)

    d_wd_parts = [dot_tn(a, g_two_low).astype(BF16) for a in acts]
    g_two_low, d_wd_parts = lax.optimization_barrier((g_two_low, d_wd_parts))
    wd_own, wd_far = to_pair(d_wd_parts)
    g_pre = [(dot_nt(g_two_low, w) * s).astype(BF16) for w, s in zip(wd, slopes)]
    g_pre, wd_far = lax.optimization_barrier((g_pre, wd_far))
    d_wd = add_far(wd_own, wd_far).astype(BF16)
    d_wu_parts = [dot_tn(hidden, g).astype(BF16) for g in g_pre]
    d_bu = [jnp.sum(g.astype(F32), axis=0) for g in g_pre]
    g_pre, d_wu_parts = lax.optimization_barrier((g_pre, d_wu_parts))
    wu_own, wu_far = to_pair(d_wu_parts)
    g_normed = g_two + sum(dot_nt(g, w) for g, w in zip(g_pre, wu))
    g_one = norm_back(g_normed, normal1, rstd1, gain1)
    d_ln1_gain = jnp.sum(g_normed * normal1, axis=0)
    d_ln1_bias = jnp.sum(g_normed, axis=0)
    g_one_low = g_one.astype(BF16)
    d_b_out = jnp.sum(g_one_low.astype(F32), axis=0)
    g_ctx_parts = [dot_nt(g_one_low, w).astype(BF16) for w in wo]
    g_one_low, g_ctx_parts = lax.optimization_barrier((g_one_low, g_ctx_parts))
    g_ctx = jnp.concatenate(
        [g_ctx_parts[0]] + [swap(g_ctx_parts[m], m) for m in range(1, count)], axis=0
    )
    tail = -(-(cols + 8) // (16 * group)) * (16 * group) - cols
    small = [d_b_out, d_ln1_gain, d_ln1_bias, d_b_down, d_ln2_gain, d_ln2_bias]
    d_wo_parts = [
        jnp.concatenate(
            [dot_tn(c, g_one_low), jnp.stack([d] + small), jnp.zeros((tail - 7, width), F32)], axis=0
        ).astype(BF16)
        for c, d in zip(ctx_own, d_bu)
    ]
    wo_own, wo_far = to_pair(d_wo_parts)
    uo_own = jnp.concatenate([wu_own, wo_own], axis=0)
    uo_far = jnp.concatenate([wu_far, wo_far], axis=0)
    g_ctx, uo_far = lax.optimization_barrier((g_ctx, uo_far))
    d_uo = add_far(uo_own, uo_far).astype(BF16)

    dq, dk, dv = attend_back(block_perm, meet, q, k, v, g_ctx, ctx, segc, segr, lse)
    d_bqv = jnp.concatenate([jnp.sum(d.astype(F32), axis=0) for d in (dq, dv)])
    fill = -(-(3 * cols + 1) // (16 * group)) * (16 * group) - 3 * cols
    d_qkv = jnp.concatenate(
        [dot_tn(d, x_all).astype(BF16) for d in (dq, dk, dv)]
        + [jnp.pad(d_bqv[None], ((0, fill - 1), (0, width - 2 * cols))).astype(BF16)],
        axis=0,
    )
    dq, dk, dv, d_qkv = lax.optimization_barrier((dq, dk, dv, d_qkv))
    part = dot_nt(dq, w_qkv[0]) + dot_nt(dk, w_qkv[1]) + dot_nt(dv, w_qkv[2])
    part = part.astype(BF16)
    in_own, in_far = to_pair([part[m * rows : (m + 1) * rows] for m in range(count)])
    grad_tokens = (g_one + add_far(in_own, in_far)).astype(BF16)

    d_qkv = sum_dp(d_qkv).astype(F32)
    d_uo = sum_dp(d_uo).astype(F32)
    d_wd = lax.psum(d_wd, "dp").astype(F32)
    small = d_uo[width + cols :]
    d_bqv = d_qkv[3 * cols, : 2 * cols].reshape(2, cols)
    d_qkv = d_qkv[: 3 * cols].reshape(3, cols, width).transpose(0, 2, 1)
    return (
        output,
        grad_tokens,
        d_qkv,
        d_bqv,
        d_uo[width : width + cols],
        small[1],
        small[2],
        small[3],
        d_uo[:width],
        small[0],
        d_wd,
        small[4],
        small[5],
        small[6],
    )


def solution(mesh):
    placed = (
        P(("dp", "tensor"), None),
        P("dp", None),
        P("tensor"),
        P(None, None, "tensor"),
        P(None, "tensor"),
        P("tensor", None),
        P(),
        P(),
        P(),
        P(None, "tensor"),
        P("tensor"),
        P("tensor", None),
        P(),
        P(),
        P(),
        P(("dp", "tensor"), None),
    )
    return jax.shard_map(
        layer,
        mesh=mesh,
        in_specs=placed,
        out_specs=(
            P(("dp", "tensor"), None),
            P(("dp", "tensor"), None),
            P(None, None, "tensor"),
            P(None, "tensor"),
            P("tensor", None),
            P(),
            P(),
            P(),
            P(None, "tensor"),
            P("tensor"),
            P("tensor", None),
            P(),
            P(),
            P(),
        ),
        check_vma=False,
    )
```

```python
import jax
import jax.numpy as jnp
from jax import lax
from jax.experimental import pallas as pl
from jax.experimental.pallas import tpu as pltpu
from jax.sharding import PartitionSpec as P

HEAD_SIZE = 64
SCALE = HEAD_SIZE ** (-0.5)
EPSILON = 1e-05
NEG = -1e30
TQ = 256
TK = 512
TM = 256
INV_ROOT_TAU = 0.3989422804014327
F32 = jnp.float32
BF16 = jnp.bfloat16


def dot_nt(a, b):
    return lax.dot_general(a, b, (((1,), (1,)), ((), ())), preferred_element_type=F32)


def dot_tn(a, b):
    return lax.dot_general(a, b, (((0,), (0,)), ((), ())), preferred_element_type=F32)


def dot_nn(a, b):
    return lax.dot_general(a, b, (((1,), (0,)), ((), ())), preferred_element_type=F32)


def head_mask(rows, cols, head):
    lane = lax.broadcasted_iota(jnp.int32, (rows, cols), 1)
    return (lane >= head * HEAD_SIZE) & (lane < (head + 1) * HEAD_SIZE)


def attend_kernel(
    perm_ref, meet_ref, x0, x1, x2, x3, w_ref, b_ref, segc_ref, segr_ref,
    q_ref, k_ref, v_ref, c0, c1, c2, c3, lse_ref, m_s, l_s, acc_s, ctx_s, turned_s,
):
    heads = perm_ref.shape[0]
    seq, cols = q_ref.shape
    rows = x0.shape[0]
    q_tiles = seq // TQ
    half_q = q_tiles // 2
    half_k = seq // TK // 2
    for r, x_ref in enumerate((x0, x1, x2, x3)):
        here = slice(r * rows, (r + 1) * rows)
        x = x_ref[...]
        q_ref[here, :] = (dot_nt(x, w_ref[0]) + b_ref[0:1, :]).astype(BF16)
        k_ref[here, :] = dot_nt(x, w_ref[1]).astype(BF16)
        value = dot_nt(x, w_ref[2]) + b_ref[1:2, :]
        v_ref[here, :] = value.astype(BF16)
        turned_s[r, :, :] = jnp.transpose(value).astype(BF16)

    def tile(i, carry):
        row0 = pl.multiple_of(i * TQ, TQ)
        block = i // half_q
        q_all = q_ref[pl.ds(row0, TQ), :].astype(F32) * SCALE
        seg_q = segr_ref[pl.ds(i // (TK // TQ), 1), :]
        seg_q = jnp.where(i % 2 == 0, seg_q[:, :TQ], seg_q[:, TQ:])
        m_s[...] = jnp.zeros_like(m_s)
        l_s[...] = jnp.ones_like(l_s)
        acc_s[...] = jnp.zeros_like(acc_s)
        for h in range(heads):
            here = slice(h * HEAD_SIZE, (h + 1) * HEAD_SIZE)
            q_h = jnp.where(head_mask(TQ, cols, h), q_all, 0.0).astype(BF16)
            key_block = jnp.where(perm_ref[h] == 1, 1 - block, block)
            for j in range(half_k):
                kt = key_block * half_k + j

                @pl.when(meet_ref[i, kt] == 1)
                def _():
                    key0 = pl.multiple_of(kt * TK, TK)
                    seg_k = segc_ref[pl.ds(key0, TK), 0:1]
                    s = dot_nt(k_ref[pl.ds(key0, TK), :], q_h)
                    s = jnp.where(seg_k == seg_q, s, NEG)
                    m_old = m_s[h : h + 1, :]
                    m_new = jnp.maximum(m_old, jnp.max(s, axis=0, keepdims=True))
                    alpha = jnp.exp(m_old - m_new)
                    p = jnp.exp(s - m_new)
                    l_s[h : h + 1, :] = alpha * l_s[h : h + 1, :] + jnp.sum(p, axis=0, keepdims=True)
                    part = dot_nn(turned_s[kt, here, :], p.astype(BF16))
                    acc_s[here, :] = alpha * acc_s[here, :] + part
                    m_s[h : h + 1, :] = m_new

            acc_s[here, :] = acc_s[here, :] / l_s[h : h + 1, :]
        lse_ref[i] = m_s[...] + jnp.log(l_s[...])
        ctx_s[pl.ds(row0, TQ), :] = jnp.transpose(acc_s[...]).astype(BF16)
        return carry

    lax.fori_loop(0, q_tiles, tile, 0)
    for r, c_ref in enumerate((c0, c1, c2, c3)):
        c_ref[...] = ctx_s[r * rows : (r + 1) * rows, :]


def attend_back_kernel(
    perm_ref, meet_ref, x0, x1, x2, x3, q_ref, k_ref, v_ref, g0, g1, g2, g3, c0, c1, c2, c3,
    segc_ref, segr_ref, lse_ref, dq_ref, dk_ref, dv_ref, dw_ref, dq_s, dk_s, dv_s, g_s, gc_s,
):
    heads = perm_ref.shape[0]
    seq, cols = q_ref.shape
    rows, width = x0.shape
    q_tiles = seq // TQ
    half_q = q_tiles // 2
    half_k = seq // TK // 2
    dk_s[...] = jnp.zeros_like(dk_s)
    dv_s[...] = jnp.zeros_like(dv_s)
    for r, (g_ref, c_ref) in enumerate(zip((g0, g1, g2, g3), (c0, c1, c2, c3))):
        here = slice(r * rows, (r + 1) * rows)
        g_s[here, :] = g_ref[...]
        gc_s[here, :] = g_ref[...].astype(F32) * c_ref[...].astype(F32)

    def tile(i, carry):
        row0 = pl.multiple_of(i * TQ, TQ)
        block = i // half_q
        q_all = q_ref[pl.ds(row0, TQ), :].astype(F32) * SCALE
        g_all = g_s[pl.ds(row0, TQ), :]
        gc_t = jnp.transpose(gc_s[pl.ds(row0, TQ), :])
        seg_q = segr_ref[pl.ds(i // (TK // TQ), 1), :]
        seg_q = jnp.where(i % 2 == 0, seg_q[:, :TQ], seg_q[:, TQ:])
        out = jnp.zeros((TQ, cols), F32)
        for h in range(heads):
            mask = head_mask(TQ, cols, h)
            q_h = jnp.where(mask, q_all, 0.0).astype(BF16)
            g_h = jnp.where(mask, g_all, jnp.zeros_like(g_all))
            delta = jnp.sum(gc_t[h * HEAD_SIZE : (h + 1) * HEAD_SIZE, :], axis=0, keepdims=True)
            lse = lse_ref[i, h : h + 1, :]
            key_block = jnp.where(perm_ref[h] == 1, 1 - block, block)
            dq_s[...] = jnp.zeros_like(dq_s)
            for j in range(half_k):
                kt = key_block * half_k + j

                @pl.when(meet_ref[i, kt] == 1)
                def _():
                    key0 = pl.multiple_of(kt * TK, TK)
                    keys = k_ref[pl.ds(key0, TK), :]
                    seg_k = segc_ref[pl.ds(key0, TK), 0:1]
                    s = dot_nt(keys, q_h)
                    p = jnp.exp(jnp.where(seg_k == seg_q, s - lse, NEG))
                    dp = dot_nt(v_ref[pl.ds(key0, TK), :], g_h)
                    ds = (p * (dp - delta)).astype(BF16)
                    dv_s[pl.ds(key0, TK), :] += dot_nn(p.astype(BF16), g_h)
                    dk_s[pl.ds(key0, TK), :] += dot_nn(ds, q_h)
                    dq_s[...] += dot_tn(ds, keys)

            out = jnp.where(mask, dq_s[...], out)
        dq_ref[pl.ds(row0, TQ), :] = (out * SCALE).astype(BF16)
        return carry

    lax.fori_loop(0, q_tiles, tile, 0)
    dk_ref[...] = dk_s[...].astype(BF16)
    dv_ref[...] = dv_s[...].astype(BF16)
    for c, d_ref in enumerate((dq_ref, dk_ref, dv_ref)):
        total = jnp.zeros((cols, width), F32)
        for r, x_ref in enumerate((x0, x1, x2, x3)):
            total += dot_tn(d_ref[r * rows : (r + 1) * rows, :], x_ref[...])
        dw_ref[c * cols : (c + 1) * cols, :] = total.astype(BF16)
    fill = dw_ref.shape[0] - 3 * cols
    row = lax.broadcasted_iota(jnp.int32, (fill, cols), 0)
    sums = [jnp.sum(d_ref[...].astype(F32), axis=0, keepdims=True) for d_ref in (dq_ref, dv_ref)]
    dw_ref[3 * cols :, :] = jnp.zeros((fill, width), BF16)
    dw_ref[3 * cols :, 0:cols] = jnp.where(row == 0, sums[0], jnp.where(row == 1, sums[1], 0.0)).astype(BF16)


def mlp_fwd_kernel(
    x_ref, c0, c1, c2, c3, p0, p1, p2, p3, d0, d1, d2, d3, vec_ref, cot_ref,
    out_ref, hid_ref, nrm_ref, rstd_ref, slope_ref, g_ref, glow_ref, sum_ref, w0, w1, w2, w3, act_s,
):
    rows, width = x_ref.shape
    cols = c0.shape[1]
    b_out, gain1, bias1, b_down, gain2, bias2 = (vec_ref[n : n + 1, :] for n in range(6))
    packs, downs = (p0, p1, p2, p3), (d0, d1, d2, d3)
    sums = [jnp.zeros((1, width), F32) for _ in range(3)]
    for t in range(rows // TM):
        here = slice(t * TM, (t + 1) * TM)
        attended = b_out
        for c_ref, p_ref in zip((c0, c1, c2, c3), packs):
            attended = attended + dot_nn(c_ref[here, :], p_ref[0:cols, :])
        normal1, rstd1 = norm_parts(x_ref[here, :].astype(F32) + attended)
        nrm_ref[here, :] = normal1
        rstd_ref[here, :] = jnp.broadcast_to(rstd1, (TM, 128))
        normed = normal1 * gain1 + bias1
        hidden = normed.astype(BF16)
        hid_ref[here, :] = hidden
        resid = normed + b_down
        for m in range(4):
            pre = dot_nn(hidden, packs[m][cols : cols + width, :])
            pre = pre + packs[m][cols + width : cols + width + 16, :][0:1, :].astype(F32)
            cdf = 0.5 * (1.0 + lax.erf(pre * (2.0 ** -0.5)))
            act = (pre * cdf).astype(BF16)
            act_s[m, here, :] = act
            slope_ref[m, here, :] = (cdf + pre * (jnp.exp(-0.5 * pre * pre) * INV_ROOT_TAU)).astype(BF16)
            resid = resid + dot_nn(act, downs[m][...])
        normal2, rstd2 = norm_parts(resid)
        out_ref[here, :] = (normal2 * gain2 + bias2).astype(BF16)
        cot = cot_ref[here, :].astype(F32)
        g_two = norm_back(cot, normal2, rstd2, gain2)
        low = g_two.astype(BF16)
        g_ref[here, :] = g_two
        glow_ref[here, :] = low
        for n, value in enumerate((low.astype(F32), cot * normal2, cot)):
            sums[n] = sums[n] + jnp.sum(value, axis=0, keepdims=True)
    for n in range(3):
        sum_ref[n : n + 1, :] = sums[n]
    low = glow_ref[...]
    for m, w_ref in enumerate((w0, w1, w2, w3)):
        w_ref[...] = dot_tn(act_s[m], low).astype(BF16)


def mlp_mid_kernel(glow_ref, slope_ref, d0, d1, d2, d3, pre_ref):
    for m, d_ref in enumerate((d0, d1, d2, d3)):
        pre_ref[m] = (dot_nt(glow_ref[...], d_ref[...]) * slope_ref[m].astype(F32)).astype(BF16)


def mlp_back_kernel(
    g_ref, pre_ref, nrm_ref, rstd_ref, p0, p1, p2, p3, vec_ref, one_ref, low_ref, y0, y1, y2, y3, sum_ref
):
    rows, width = g_ref.shape
    cols = y0.shape[1]
    gain1 = vec_ref[1:2, :]
    packs = (p0, p1, p2, p3)
    sums = [jnp.zeros((1, width), F32) for _ in range(7)]
    for t in range(rows // TM):
        here = slice(t * TM, (t + 1) * TM)
        g_normed = g_ref[here, :]
        for m in range(4):
            pre = pre_ref[m, here, :]
            sums[3 + m] = sums[3 + m] + jnp.sum(pre.astype(F32), axis=0, keepdims=True)
            g_normed = g_normed + dot_nt(pre, packs[m][cols : cols + width, :])
        normal = nrm_ref[here, :]
        g_one = norm_back(g_normed, normal, rstd_ref[here, 0:1], gain1)
        low = g_one.astype(BF16)
        one_ref[here, :] = g_one
        low_ref[here, :] = low
        for n, value in enumerate((low.astype(F32), g_normed * normal, g_normed)):
            sums[n] = sums[n] + jnp.sum(value, axis=0, keepdims=True)
        for m, y_ref in enumerate((y0, y1, y2, y3)):
            y_ref[here, :] = dot_nt(low, packs[m][0:cols, :]).astype(BF16)
    for n in range(7):
        sum_ref[n : n + 1, :] = sums[n]


def mlp_grad_kernel(hid_ref, pre_ref, low_ref, c0, c1, c2, c3, back_ref, fwd_ref, u0, u1, u2, u3):
    width = low_ref.shape[1]
    cols = c0.shape[1]
    fill = u0.shape[0] - width - cols
    row = lax.broadcasted_iota(jnp.int32, (fill, width), 0)
    shared = [back_ref[0:1, :], back_ref[1:2, :], back_ref[2:3, :], fwd_ref[0:1, :], fwd_ref[1:2, :], fwd_ref[2:3, :]]
    for m, (c_ref, u_ref) in enumerate(zip((c0, c1, c2, c3), (u0, u1, u2, u3))):
        u_ref[0:width, :] = dot_tn(hid_ref[...], pre_ref[m]).astype(BF16)
        u_ref[width : width + cols, :] = dot_tn(c_ref[...], low_ref[...]).astype(BF16)
        block = jnp.where(row == 0, back_ref[3 + m : 4 + m, :], 0.0)
        for n, value in enumerate(shared):
            block = jnp.where(row == n + 1, value, block)
        u_ref[width + cols :, :] = block.astype(BF16)


def in_parts_kernel(dq_ref, dk_ref, dv_ref, w_ref, o0, o1, o2, o3):
    rows = o0.shape[0]
    for r, o_ref in enumerate((o0, o1, o2, o3)):
        here = slice(r * rows, (r + 1) * rows)
        total = dot_nn(dq_ref[here, :], w_ref[0]) + dot_nn(dk_ref[here, :], w_ref[1])
        o_ref[...] = (total + dot_nn(dv_ref[here, :], w_ref[2])).astype(BF16)


def whole(kernel, outs, args, smem=0, scratch=(), room=24):
    vmem = pl.BlockSpec(memory_space=pltpu.VMEM)
    shape = [jax.ShapeDtypeStruct(dims, kind) for dims, kind in outs]
    return pl.pallas_call(
        kernel,
        in_specs=[pl.BlockSpec(memory_space=pltpu.SMEM)] * smem + [vmem] * (len(args) - smem),
        out_specs=[vmem] * len(shape),
        out_shape=shape,
        scratch_shapes=[pltpu.VMEM(dims, kind) for dims, kind in scratch],
        compiler_params=pltpu.CompilerParams(vmem_limit_bytes=room * 1024 * 1024),
    )(*args)


def norm_parts(resid):
    centered = resid - jnp.mean(resid, axis=-1, keepdims=True)
    rstd = lax.rsqrt(jnp.mean(centered * centered, axis=-1, keepdims=True) + EPSILON)
    return centered * rstd, rstd


def norm_back(cot, normal, rstd, gain):
    dn = cot * gain
    return rstd * (
        dn - jnp.mean(dn, axis=-1, keepdims=True) - normal * jnp.mean(dn * normal, axis=-1, keepdims=True)
    )


def layer(
    tokens,
    segments,
    block_perm,
    w_qkv,
    b_qv,
    w_out,
    b_out,
    ln1_gain,
    ln1_bias,
    w_up,
    b_up,
    w_down,
    b_down,
    ln2_gain,
    ln2_bias,
    cotangent,
):
    count = lax.axis_size("tensor")
    place = lax.axis_index("tensor")
    group = lax.axis_size("dp")
    member = lax.axis_index("dp")
    rows, width = tokens.shape
    cols = w_out.shape[0]
    units = w_up.shape[1]

    def swap(value, mask):
        return lax.ppermute(value, "tensor", [(i, i ^ mask) for i in range(count)])

    def swap_dp(value, mask):
        return lax.ppermute(value, "dp", [(i, i ^ mask) for i in range(group)])

    def after(value, *others):
        return lax.optimization_barrier((value,) + others)[0]

    masks = [1 << i for i in range(group.bit_length() - 1)]

    def fold_dp(value, mask):
        half = value.shape[-2] // 2
        bit = (member // mask) % 2
        sent = lax.dynamic_slice_in_dim(value, (1 - bit) * half, half, value.ndim - 2)
        kept = lax.dynamic_slice_in_dim(value, bit * half, half, value.ndim - 2)
        got = swap_dp(sent, mask)
        return (kept.astype(F32) + got.astype(F32)).astype(BF16)

    def join_dp(value, mask):
        got = swap_dp(value, mask)
        first = (member // mask) % 2 == 0
        return jnp.concatenate([jnp.where(first, value, got), jnp.where(first, got, value)], axis=0)

    def sum_dp(value):
        for mask in masks:
            value = fold_dp(value, mask)
        for mask in reversed(masks):
            value = join_dp(value, mask)
        return value

    slab = units // group
    wd_slab = lax.dynamic_slice_in_dim(w_down, member * slab, slab, 0)
    x2 = swap(tokens, 2)
    x1 = swap(tokens, 1)
    wd_slab = swap(wd_slab, 2)
    wd1 = swap(w_down, 1)
    x3 = swap(x2, 1)

    seq = 4 * rows
    w_rows = w_qkv.transpose(0, 2, 1)
    packed_a = jnp.concatenate([w_out, w_up, jnp.broadcast_to(b_up[None], (16, units))], axis=0)
    vectors = jnp.concatenate(
        [z[None].astype(F32) for z in (b_out, ln1_gain, ln1_bias, b_down, ln2_gain, ln2_bias, b_out, b_out)]
    )
    seg4 = segments[0].reshape(count, rows)
    seg_row = jnp.concatenate(
        [lax.dynamic_slice_in_dim(seg4, place ^ m, 1, 0) for m in range(count)], axis=0
    ).reshape(seq)
    segc = jnp.broadcast_to(seg_row[:, None], (seq, 128))
    segr = seg_row.reshape(seq // TK, TK)
    q_lo, q_hi = (f(seg_row.reshape(seq // TQ, TQ), axis=1) for f in (jnp.min, jnp.max))
    k_lo, k_hi = (f(segr, axis=1) for f in (jnp.min, jnp.max))
    meet = ((q_lo[:, None] <= k_hi[None]) & (k_lo[None] <= q_hi[:, None])).astype(jnp.int32)

    wd_slab, packed_a, vectors, segc, segr, meet = lax.optimization_barrier(
        (wd_slab, packed_a, vectors, segc, segr, meet)
    )
    wd2 = lax.all_gather(wd_slab, "dp", axis=0, tiled=True)
    packed_a = after(packed_a, x2)
    pa2 = swap(packed_a, 2)
    pa1 = swap(packed_a, 1)

    xs = (tokens, x1, x2, x3)
    q, k, v, *rest = whole(
        attend_kernel,
        [((seq, cols), BF16)] * 3 + [((rows, cols), BF16)] * 4 + [((seq // TQ, 8, TQ), F32)],
        (block_perm, meet, *xs, w_rows, b_qv.astype(F32), segc, segr),
        smem=2,
        scratch=[((8, TQ), F32), ((8, TQ), F32), ((cols, TQ), F32), ((seq, cols), BF16), ((count, cols, rows), BF16)],
    )
    ctx, lse = rest[:4], rest[4]

    ctx_own = [ctx[0]] + [swap(ctx[m], m) for m in range(1, count)]
    pa3 = swap(after(pa2, ctx[0]), 1)
    wd3 = swap(after(wd2, ctx[0]), 1)
    packs = (packed_a, pa1, pa2, pa3)
    downs = (w_down, wd1, wd2, wd3)
    token_f, token_b = ((rows, width), F32), ((rows, width), BF16)
    wide = ((count, rows, units), BF16)
    output, hidden, normal1, rstd1, slopes, g_two, g_two_low, sums_f, *d_wd = whole(
        mlp_fwd_kernel,
        [token_b, token_b, token_f, ((rows, 128), F32), wide, token_f, token_b, ((8, width), F32)]
        + [((units, width), BF16)] * 4,
        (tokens, *ctx_own, *packs, *downs, vectors, cotangent),
        scratch=[wide],
        room=40,
    )

    def add_low(one, two):
        return (one.astype(F32) + two.astype(F32)).astype(BF16)

    def to_pair(parts):
        near = swap(parts[1], 1)
        far = swap(parts[3], 1)
        return add_low(parts[0], near), add_low(parts[2], far)

    wd_own, wd_far = to_pair(d_wd)
    (g_pre,) = whole(mlp_mid_kernel, [wide], (g_two_low, slopes, *downs))
    wd_pair, g_pre = lax.optimization_barrier((jnp.stack([wd_own, wd_far]), g_pre))
    wd_half = fold_dp(wd_pair, masks[0])
    g_one, g_one_low, *rest = whole(
        mlp_back_kernel,
        [token_f, token_b] + [((rows, cols), BF16)] * 4 + [((8, width), F32)],
        (g_two, g_pre, normal1, rstd1, *packs, vectors),
    )
    g_ctx_parts, sums_b = rest[:4], rest[4]
    g_ctx = [g_ctx_parts[0]] + [swap(g_ctx_parts[m], m) for m in range(1, count)]
    tail = -(-(cols + 8) // (16 * group)) * (16 * group)
    d_uo = whole(
        mlp_grad_kernel, [((width + tail, units), BF16)] * 4, (hidden, g_pre, g_one_low, *ctx_own, sums_b, sums_f)
    )
    uo_own, uo_far = to_pair(d_uo)
    uo_far, g_ctx, uo_own = lax.optimization_barrier((uo_far, g_ctx, uo_own))
    uo_got = swap(uo_far, 2)

    fill = -(-(3 * cols + 2) // (16 * group)) * (16 * group)
    dq, dk, dv, d_qkv = whole(
        attend_back_kernel,
        [((seq, cols), BF16)] * 3 + [((fill, width), BF16)],
        (block_perm, meet, *xs, q, k, v, *g_ctx, *ctx, segc, segr, lse),
        smem=2,
        scratch=[((TQ, cols), F32), ((seq, cols), F32), ((seq, cols), F32), ((seq, cols), BF16), ((seq, cols), F32)],
    )
    parts = whole(in_parts_kernel, [token_b] * 4, (dq, dk, dv, w_rows))
    in_own, in_far = to_pair(parts)
    grad_tokens = (g_one + in_own.astype(F32) + swap(in_far, 2).astype(F32)).astype(BF16)

    for mask in masks[1:]:
        wd_half = fold_dp(wd_half, mask)
    d_wd = add_low(wd_half[0], swap(wd_half[1], 2))
    for mask in reversed(masks):
        d_wd = join_dp(d_wd, mask)
    d_uo = sum_dp(add_low(uo_own, uo_got))
    d_qkv = lax.psum(d_qkv, "dp")
    small = d_uo[width + cols : width + cols + 8].astype(F32)
    return (
        output,
        grad_tokens,
        d_qkv[: 3 * cols].astype(F32).reshape(3, cols, width).transpose(0, 2, 1),
        d_qkv[3 * cols : 3 * cols + 2, :cols].astype(F32),
        d_uo[width : width + cols].astype(F32),
        small[1],
        small[2],
        small[3],
        d_uo[:width].astype(F32),
        small[0],
        d_wd.astype(F32),
        small[4],
        small[5],
        small[6],
    )


def solution(mesh):
    placed = (
        P(("dp", "tensor"), None),
        P("dp", None),
        P("tensor"),
        P(None, None, "tensor"),
        P(None, "tensor"),
        P("tensor", None),
        P(),
        P(),
        P(),
        P(None, "tensor"),
        P("tensor"),
        P("tensor", None),
        P(),
        P(),
        P(),
        P(("dp", "tensor"), None),
    )
    return jax.shard_map(
        layer,
        mesh=mesh,
        in_specs=placed,
        out_specs=(
            P(("dp", "tensor"), None),
            P(("dp", "tensor"), None),
            P(None, None, "tensor"),
            P(None, "tensor"),
            P("tensor", None),
            P(),
            P(),
            P(),
            P(None, "tensor"),
            P("tensor"),
            P("tensor", None),
            P(),
            P(),
            P(),
        ),
        check_vma=False,
    )
```
